1024 devices in a mesh: dp: 32 (over z, x_hi), expert: 32 (over x_lo, y, core).
Axes of the slice: x: 4 (x_hi: 2, x_lo: 2; x = x_hi * 2 + x_lo), y: 8, z: 16, core: 2. Of those that a mesh axis runs over, the one named last changes fastest.
Arguments:
- grad_output: bfloat16 [4096, 6144], P('expert', 'dp'), may hold values from -6 to 6
- gate_probs: float32 [4096, 4], P('expert'), may hold values from 0.05 to 1
- routing: int32 [4096, 4], P('expert'), may hold values from 0 to 127, all different within a row; in each aligned block of 128 rows (0 to 127, 128 to 255, ...) at most 5 rows name the same one
- old_weights: bfloat16 [128, 1024, 6144], P('expert', None, 'dp'), may hold values from -0.1875 to 0.1875
- old_slot_expert: int32 [128], replicated, may hold values from 0 to 127, each once
- new_slot_expert: int32 [128], replicated, may hold values from 0 to 127, each once
- saved_hidden: bfloat16 [128, 160, 1024], P('expert'), may hold values from -6 to 6
- shared_hidden: bfloat16 [4096, 1024], P('expert'), may hold values from -6 to 6
- shared_weight: bfloat16 [1024, 6144], P('expert', 'dp'), may hold values from -0.1875 to 0.1875
Outputs:
- expert_weight_grad: bfloat16 [128, 1024, 6144], P('expert', None, 'dp')
- expert_hidden_grad: bfloat16 [128, 160, 1024], P('expert', 'dp')
- shared_hidden_grad: bfloat16 [4096, 1024], P('expert', 'dp')
- shared_weight_grad: bfloat16 [1024, 6144], P('expert', 'dp')
The draws below stay inside these ranges and needn't reach their ends.
Inputs may be any that keep to these rules, and one draw needn't show every extreme that they name: `routing`: each row names 4 different experts. Among the 128 rows of one group no expert is named by more than 5 rows, a bound that some block reaches of them. `old_slot_expert`: A permutation of the experts. `new_slot_expert`: A permutation of the experts.
All inputs are finite; a program needn't handle non-finite values.
Results may differ from the reference program's by a relative error of at most 0.023.
Values may be sent and summed in bfloat16 or wider, within the bound.
No kernel may reach another device: no remote copies, remote signals or barrier semaphores. Data moves between devices by JAX's collectives and lax.ppermute only.
A program may use at most 32 MiB of HBM per device.

```python
import math
import jax
import jax.numpy as jnp
import numpy as np
from jax import lax

D = 6144
FF_E = 1024
HS = 1024
TOP = 4
TOK_GRP = 128
EXPERTS = 128
CAP = 5
TOKENS = 4096
N_DP = 32
N_EXPERT = 32


def block_scale(rng, extent, shards, smallest, largest):
    def one(dim, blocks):
        draws = jax.random.uniform(jax.random.fold_in(jax.random.fold_in(rng, 6), dim), (blocks,), jnp.float32, smallest / len(shards), largest / len(shards))
        return jnp.repeat(jnp.exp(draws), extent[dim] // blocks).reshape((-1,) + (1,) * (len(extent) - dim - 1))

    factor_of = one(*shards[0])
    for cut in shards[1:]:
        factor_of = factor_of * one(*cut)
    return factor_of


def shared_out(own_key, own, number, rows, amount, top, bound, skew):
    order = jax.random.permutation(own_key, amount)
    packed, ordinary = portions_of(amount, rows * top, bound, skew, True), portions_of(amount, rows * top, bound, skew, False)
    places = jnp.arange(amount)

    def named(tallies, rotation):
        used = int((tallies > 0).sum())
        fixed = max(1, used // 4)
        shifted = fixed + (places - fixed + rotation * (used - fixed)) % max(1, amount - fixed)
        return jnp.zeros((amount,), jnp.int32).at[order[jnp.where(places < fixed, places, shifted)]].set(jnp.asarray(tallies, jnp.int32))

    tallies = jnp.where(number % 4 == 0, named(packed, number // 4), named(ordinary, number - number // 4 - 1))
    mixed = jax.random.permutation(jax.random.fold_in(own, 3), amount)
    source_of, taker = mixed[0:amount // 2 * 2:2], mixed[1:amount // 2 * 2:2]
    room = jnp.minimum(tallies[source_of] - 1, bound - tallies[taker]) // 2
    room = jnp.where((source_of == order[0]) | (taker == order[0]) | (tallies[taker] == 0), 0, jnp.maximum(room, 0))
    shifted = jax.random.randint(jax.random.fold_in(own, 4), (amount // 2,), 0, 1 << 20) % (room + 1)
    tallies = tallies.at[source_of].add(-shifted).at[taker].add(shifted)
    items = jnp.searchsorted(jnp.cumsum(tallies), jnp.arange(rows * top), side="right").astype(jnp.int32)
    table = items.reshape(top, rows).T
    table = table[jax.random.permutation(jax.random.fold_in(own, 1), rows)]
    rotation = jax.random.randint(jax.random.fold_in(own, 2), (rows, 1), 0, top)
    return jnp.take_along_axis(table, (jnp.arange(top)[None, :] + rotation) % top, axis=1)


def portions_of(number_of, total, bound, lean, full):
    portions = [(1 << 20) // math.isqrt(rank ** lean) + 1 for rank in range(1, number_of + 1)]
    largest = bound if full else min(bound, max(-(-total // number_of), total * portions[0] // sum(portions)))
    least = 1 if total - largest >= number_of - 1 else 0
    holding, surplus = [largest] + [least] * (number_of - 1), total - largest - least * (number_of - 1)
    while surplus > 0:
        candidates = [i for i in range(1, number_of) if holding[i] < largest] or [i for i in range(1, number_of) if holding[i] < bound]
        whole, remaining = sum([portions[i] for i in candidates]), surplus
        for i in candidates:
            more = min(bound - holding[i], max(1, remaining * portions[i] // whole), surplus)
            holding[i] = holding[i] + more
            surplus = surplus - more
    return np.array(holding)


def bell_draw(own_key, extent, deviation, reach, pieces=(), kind=jnp.bfloat16):
    result = deviation * jax.random.normal(own_key, extent, jnp.float32)
    if pieces:
        result = result * block_scale(own_key, extent, pieces, -0.22, 0.18)
    return jnp.clip(result, -reach, reach).astype(kind)


def setup_inputs(seed: int = 0) -> dict:
    arg_keys = jax.random.split(jax.random.key(seed), 10)
    grad_output = bell_draw(arg_keys[0], (TOKENS, D), 1.0, 6.0, ((0, 32), (1, 32)))
    gate_probs = jnp.clip(jnp.exp(math.log(1.0) - 2.9957323 * jax.random.uniform(arg_keys[1], (TOKENS, TOP), jnp.float32) ** block_scale(arg_keys[1], (TOKENS, TOP), ((0, 32),), -0.2, 0.2)), 0.05, 1.0)
    routing_keys = jax.random.split(jax.random.fold_in(arg_keys[2], 1), TOKENS // TOK_GRP)
    routing_turns = jax.random.permutation(jax.random.fold_in(arg_keys[2], 3), TOKENS // TOK_GRP)
    routing = jax.vmap(lambda own, number: shared_out(jax.random.fold_in(arg_keys[2], 2), own, number, TOK_GRP, EXPERTS, TOP, CAP, 2))(routing_keys, routing_turns).reshape((TOKENS, TOP))
    old_weights = bell_draw(arg_keys[3], (EXPERTS, FF_E, D), FF_E ** -0.5, 0.1875, ((0, 32), (2, 32)))
    old_slot_expert = jax.random.permutation(arg_keys[4], EXPERTS).astype(jnp.int32)
    new_slot_expert = jax.random.permutation(arg_keys[5], EXPERTS).astype(jnp.int32)
    saved_hidden = bell_draw(arg_keys[6], (EXPERTS, N_EXPERT * CAP, FF_E), 1.0, 6.0, ((0, 32),))
    shared_hidden = bell_draw(arg_keys[7], (TOKENS, HS), 1.0, 6.0, ((0, 32),))
    shared_weight = bell_draw(arg_keys[8], (HS, D), HS ** -0.5, 0.1875, ((0, 32), (1, 32)))
    return {"grad_output": grad_output, "gate_probs": gate_probs, "routing": routing, "old_weights": old_weights, "old_slot_expert": old_slot_expert, "new_slot_expert": new_slot_expert, "saved_hidden": saved_hidden, "shared_hidden": shared_hidden, "shared_weight": shared_weight}


def inverse_order(listing):
    labels = jnp.arange(listing.shape[0], dtype=jnp.int32)
    return jnp.sum(jnp.where(listing[None, :] == labels[:, None], labels[None, :], 0), axis=1).astype(jnp.int32)


def reference(grad_output, gate_probs, routing, old_weights, old_slot_expert, new_slot_expert, saved_hidden, shared_hidden, shared_weight):
    experts, hidden, columns = old_weights.shape
    slot_rows = saved_hidden.shape[1]
    capacity = slot_rows // N_EXPERT
    tokens, chosen = routing.shape
    tok_grp = tokens // N_EXPERT
    shared_units = shared_weight.shape[0]
    blocksize = columns // N_DP
    old_position = inverse_order(old_slot_expert)
    new_position = inverse_order(new_slot_expert)
    source_slot = jnp.take(old_position, new_slot_expert).astype(jnp.int32)
    relayed = jnp.take(old_weights, source_slot, axis=0)
    labels = jnp.arange(experts, dtype=jnp.int32)
    flattened = routing.reshape(N_EXPERT, tok_grp * chosen)
    onehot = (flattened[:, :, None] == labels[None, None, :]).astype(jnp.int32)
    earlier = jnp.cumsum(onehot, axis=1) - onehot
    ranking = jnp.sum(earlier * onehot, axis=2).astype(jnp.int32)
    slot_index = jnp.take(new_position, flattened.reshape(-1)).reshape(N_EXPERT, tok_grp * chosen).astype(jnp.int32)
    sources = jnp.arange(N_EXPERT, dtype=jnp.int32)[:, None]
    target = (slot_index * slot_rows + sources * capacity + ranking).reshape(-1).astype(jnp.int32)
    scaled = (grad_output.astype(jnp.float32)[:, None, :] * gate_probs[:, :, None]).astype(jnp.bfloat16).reshape(tokens * chosen, columns)
    routed_rows = jnp.zeros((experts * slot_rows, columns), jnp.bfloat16).at[target].set(scaled).reshape(experts, slot_rows, columns)

    def one_expert(operands):
        incoming, weight, saved = operands
        weight_grad = jnp.dot(saved.T, incoming, preferred_element_type=jnp.float32).astype(jnp.bfloat16)
        partial_value = jnp.einsum("rbc,fbc->brf", incoming.reshape(slot_rows, N_DP, blocksize).astype(jnp.float32), weight.reshape(hidden, N_DP, blocksize).astype(jnp.float32))
        rounded = lax.optimization_barrier(partial_value.astype(jnp.bfloat16)).astype(jnp.float32)
        return weight_grad, jnp.sum(rounded, axis=0).astype(jnp.bfloat16)

    expert_weight_grad, expert_hidden_grad = lax.map(one_expert, (routed_rows, relayed, saved_hidden))

    grad_blocks = jnp.transpose(grad_output.reshape(tokens, N_DP, blocksize), (1, 0, 2))
    weight_blocks = jnp.transpose(shared_weight.reshape(shared_units, N_DP, blocksize), (1, 0, 2))

    def add_block(total, operands):
        grad_part, weight_part = operands
        term = jnp.dot(grad_part, weight_part.T, preferred_element_type=jnp.float32)
        rounded = lax.optimization_barrier(term.astype(jnp.bfloat16)).astype(jnp.float32)
        return total + rounded, None

    shared_total, _ = lax.scan(add_block, jnp.zeros((tokens, shared_units), jnp.float32), (grad_blocks, weight_blocks))
    shared_hidden_grad = shared_total.astype(jnp.bfloat16)

    hidden_groups = shared_hidden.reshape(N_EXPERT, tok_grp, shared_units)
    grad_groups = grad_output.reshape(N_EXPERT, tok_grp, columns)

    def add_group(total, operands):
        hidden_part, grad_part = operands
        term = jnp.dot(hidden_part.T, grad_part, preferred_element_type=jnp.float32)
        rounded = lax.optimization_barrier(term.astype(jnp.bfloat16)).astype(jnp.float32)
        return total + rounded, None

    weight_total, _ = lax.scan(add_group, jnp.zeros((shared_units, columns), jnp.float32), (hidden_groups, grad_groups))
    shared_weight_grad = weight_total.astype(jnp.bfloat16)
    return expert_weight_grad, expert_hidden_grad, shared_hidden_grad, shared_weight_grad
```

```python
import jax
import jax.numpy as jnp
from jax import lax
from jax.experimental import pallas as pl
from jax.experimental.pallas import tpu as pltpu
from jax.sharding import Mesh
from jax.sharding import PartitionSpec as P

F32, BF16, I32 = jnp.float32, jnp.bfloat16, jnp.int32
INTERPRET = False

MESSAGE = 168


def iota(shape, dim):
    return lax.broadcasted_iota(I32, shape, dim)


def dot(a, b, a_dim=1, b_dim=0):
    return lax.dot_general(a, b, (((a_dim,), (b_dim,)), ((), ())), preferred_element_type=F32)


def call(body, out, *args, flops=0):
    outs = out if isinstance(out, tuple) else (out,)
    moved = sum(x.size * x.dtype.itemsize for x in (*args, *outs))
    return pl.pallas_call(
        body,
        out_shape=out,
        interpret=INTERPRET,
        cost_estimate=pl.CostEstimate(flops=flops, bytes_accessed=moved, transcendentals=0),
    )(*args)


def tails(grad):
    low = grad[128:192, :]
    none = jnp.zeros((64, 128), BF16)
    return jnp.concatenate([low, none], axis=0), jnp.concatenate([none, low], axis=0)


def pack_body(grad_ref, gate_ref, routing_ref, old_ref, new_ref, hidden_ref, weight_ref, out_ref):
    grad = grad_ref[...]
    first, last = tails(grad)
    head = grad[0:128, :]
    wide = (32, 24, 128)
    flat = (768, 128)
    row, lane = iota(wide, 1), iota(wide, 2)
    slot = iota(wide, 0) * 4 + lax.bitwise_and(row, 3)
    pick = jnp.where(lane == slot, 1.0, 0.0).astype(F32).reshape(flat).astype(BF16)
    rank_of_row = lax.shift_right_logical(row, 2).astype(F32).reshape(flat)
    before = jnp.where(iota((128, 128), 0) < iota((128, 128), 1), 1.0, 0.0).astype(BF16)
    routing = routing_ref[...].astype(F32)
    gates = gate_ref[...]

    def rows_for(listing_ref):
        listing = jnp.broadcast_to(listing_ref[...].astype(F32), (128, 128)).astype(BF16)
        expert = dot(pick, listing, 1, 1)
        named = jnp.zeros(flat, F32)
        gate = jnp.zeros(flat, F32)
        for k in range(4):
            match = expert == routing[k : k + 1, :]
            named = jnp.where(match, 1.0, named)
            gate = jnp.where(match, gates[k : k + 1, :], gate)
        rank = dot(named.astype(BF16), before)
        chosen = jnp.logical_and(named > 0.5, rank == rank_of_row)
        select = jnp.where(chosen, 1.0, 0.0).astype(BF16)
        scale = jnp.sum(jnp.where(chosen, gate, 0.0), axis=1, keepdims=True)
        return select, scale

    old_select, old_scale = rows_for(old_ref)
    new_select, new_scale = rows_for(new_ref)
    old_rows = (dot(old_select, head, 1, 1) * old_scale).reshape(wide)
    new_rows = (dot(new_select, head, 1, 1) * new_scale).reshape(wide)
    out_ref[:, 0:48, :] = jnp.concatenate([old_rows, new_rows], axis=1).astype(BF16)
    rest = dot(old_select, first, 1, 1) * old_scale + dot(new_select, last, 1, 1) * new_scale
    out_ref[:, 144:168, :] = rest.reshape(wide).astype(BF16)
    weight = weight_ref[...]
    out_ref[:, 48:80, :] = jnp.broadcast_to(weight[None, :, 0:128], (32, 32, 128))
    both = jnp.concatenate([weight[0:16, 128:192], weight[16:32, 128:192]], axis=1)
    out_ref[:, 80:96, :] = jnp.broadcast_to(both[None], (32, 16, 128))
    hidden = hidden_ref[...]
    out_ref[:, 96:128, :] = dot(hidden, head, 0, 1).reshape(32, 32, 128).astype(BF16)
    low = dot(hidden, first, 0, 1).reshape(32, 32, 128)[:, 0:16]
    high = dot(hidden, last, 0, 1).reshape(32, 32, 128)[:, 16:32]
    out_ref[:, 128:144, :] = (low + high).astype(BF16)


def hidden_body(message_ref, old_weights_ref, grad_ref, out_ref, shared_ref):
    grad = grad_ref[...]
    first, last = tails(grad)
    units = dot(message_ref[:, :, 48:80, :].reshape(1024, 128), grad[0:128, :]).reshape(32, 32, 128)
    pairs = message_ref[:, :, 80:96, :].reshape(512, 128)
    low, high = dot(pairs, first).reshape(32, 16, 128), dot(pairs, last).reshape(32, 16, 128)
    units = units + jnp.concatenate([low, high], axis=1)
    shared_ref[...] = units.reshape(8, 4, 32, 128).astype(BF16)
    weights = old_weights_ref[...].reshape(768, 1024)
    lane = iota((192, 128), 1)
    left = lane < 64
    own = lax.bitwise_and(iota((8, 24, 128), 1), 3).reshape(192, 128)
    wide = (8, 24, 256)
    row = iota(wide, 1) - 20
    where_to = iota(wide, 2) - iota(wide, 0) * 32 - row * 8
    where_to = jnp.where(row >= 0, where_to, -1).reshape(192, 256)

    def step(m, carry):
        heads = message_ref[:, m, 0:48, :].astype(F32)[:, 0:24, :].reshape(192, 128)
        rest = message_ref[:, m, 144:168, :].astype(F32).reshape(192, 128)
        heads_turned = pltpu.roll(heads, 64, 1)
        rest_turned = pltpu.roll(rest, 64, 1)
        blocks = []
        for e in (0, 2):
            blocks.append(jnp.where(own == e, heads, 0.0))
            blocks.append(
                jnp.where(
                    left, jnp.where(own == e, rest, 0.0), jnp.where(own == e + 1, heads_turned, 0.0)
                )
            )
            blocks.append(jnp.where(own == e + 1, jnp.where(left, heads_turned, rest_turned), 0.0))
        total = dot(jnp.concatenate(blocks, axis=1).astype(BF16), weights)
        shared = shared_ref[:, m].reshape(256, 128)
        placed = [
            dot(jnp.where(where_to == j, 1.0, 0.0).astype(BF16), shared) for j in range(8)
        ]
        total = total + jnp.concatenate(placed, axis=1)
        out_ref[m] = total.reshape(8, 24, 1024).astype(BF16)
        return carry

    lax.fori_loop(0, 4, step, 0)


def weight_body(message_ref, saved_ref, out_ref, shared_ref):
    heads = message_ref[:, 0:48, :].astype(F32)[:, 24:48, :].reshape(768, 128)
    rest = message_ref[:, 144:168, :].astype(F32).reshape(768, 128)
    rows = jnp.concatenate([heads, rest], axis=1).astype(BF16)
    line, place = iota((160, 768), 0), iota((160, 768), 1)
    group = lax.shift_right_logical(line * 205, 10)
    start = (line + group) * 4

    def step(e, carry):
        match = jnp.where(place == start + e, 1.0, 0.0).astype(BF16)
        own = dot(match, rows).astype(BF16)
        product = dot(own, saved_ref[e], 0, 0).astype(BF16)
        out_ref[e, 0:128, :] = product[0:128]
        out_ref[e, 128:192, :] = product[192:256]
        return carry

    lax.fori_loop(0, 4, step, 0)
    total = jnp.sum(message_ref[:, 96:144, :].astype(F32), axis=0)
    shared_ref[:, 0:128] = total[0:32].astype(BF16)
    tail = jnp.concatenate([total[32:48, 0:64], pltpu.roll(total[32:48], 64, 1)[:, 0:64]], axis=0)
    shared_ref[:, 128:192] = tail.astype(BF16)


def partial_body(in_ref, out_ref):
    out_ref[...] = jnp.sum(in_ref[...].astype(F32), axis=0).astype(BF16)


def spread_body(in_ref, out_ref, shared_ref):
    total = jnp.sum(in_ref[...].astype(F32), axis=0)
    for c in range(5):
        for h in range(4):
            piece = total[c * 4 : c * 4 + 4]
            at = h * 256
            both = jnp.concatenate([piece[:, at : at + 128], piece[:, at + 128 : at + 256]], axis=0)
            out_ref[c * 4 + h] = both.astype(BF16)
    out_ref[20:32] = jnp.zeros((12, 8, 128), BF16)
    units = [
        total[20 + r : 21 + r, j * 128 : (j + 1) * 128] for r in range(4) for j in range(8)
    ]
    shared_ref[...] = jnp.concatenate(units, axis=0).astype(BF16)


def permute_body(in_ref, old_ref, new_ref, out_ref):
    line, lane = iota((256, 128), 0), iota((256, 128), 1)
    slot = lax.shift_right_logical(line, 3) * 4 + lax.bitwise_and(line, 3)
    pick = jnp.where(lane == slot, 1.0, 0.0)
    wide = jnp.broadcast_to(new_ref[...].astype(F32), (256, 128)).astype(BF16)
    to = dot(pick.astype(BF16), wide, 1, 1)
    mine = jnp.broadcast_to(old_ref[...].astype(F32), (256, 128)).astype(BF16)
    source = dot(mine, pick.astype(BF16), 1, 1)
    side = lax.bitwise_and(iota((256, 256), 0), 4) == lax.bitwise_and(iota((256, 256), 1), 4)
    match = jnp.where(jnp.logical_and(to == source, side), 1.0, 0.0).astype(BF16)
    moved = dot(match, in_ref[...].reshape(256, 128))
    out_ref[...] = moved.reshape(32, 8, 128).astype(BF16)


def gather_body(in_ref, out_ref):
    for c in range(5):
        for h in range(4):
            both = in_ref[c * 4 + h].astype(F32)
            at = h * 256
            out_ref[c, :, at : at + 128] = both[0:4].astype(BF16)
            out_ref[c, :, at + 128 : at + 256] = both[4:8].astype(BF16)


def pack(grad, gates, routing, old, new, hidden, weight):
    out = jax.ShapeDtypeStruct((32, MESSAGE, 128), BF16)
    return call(pack_body, out, grad, gates, routing, old, new, hidden, weight, flops=10**9)


def hidden_terms(message, weights, grad):
    message = message.reshape(8, 4, MESSAGE, 128)
    out = jax.ShapeDtypeStruct((4, 8, 24, 1024), BF16)
    moved = sum(x.size * 2 for x in (message, weights, grad, out))
    return pl.pallas_call(
        hidden_body,
        out_shape=out,
        scratch_shapes=[pltpu.VMEM((8, 4, 32, 128), BF16)],
        interpret=INTERPRET,
        cost_estimate=pl.CostEstimate(flops=2 * 10**9, bytes_accessed=moved, transcendentals=0),
    )(message, weights, grad)


def weight_terms(message, saved):
    out = (
        jax.ShapeDtypeStruct((4, 192, 1024), BF16),
        jax.ShapeDtypeStruct((32, 192), BF16),
    )
    return call(weight_body, out, message, saved, flops=10**9)


def partial_sum(received):
    return call(partial_body, jax.ShapeDtypeStruct(received.shape[1:], BF16), received)


def spread(received):
    out = (jax.ShapeDtypeStruct((32, 8, 128), BF16), jax.ShapeDtypeStruct((32, 128), BF16))
    return call(spread_body, out, received)


def permute(received, old, new):
    return call(permute_body, jax.ShapeDtypeStruct((32, 8, 128), BF16), received, old, new)


def gather(received):
    return call(gather_body, jax.ShapeDtypeStruct((5, 4, 1024), BF16), received)


def exchange(array, axes):
    return lax.all_to_all(array, axes, 0, 0, tiled=True)


def on_device(
    grad_output,
    gate_probs,
    routing,
    old_weights,
    old_slot_expert,
    new_slot_expert,
    saved_hidden,
    shared_hidden,
    shared_weight,
):
    grad = grad_output.T
    old, new = old_slot_expert.reshape(1, 128), new_slot_expert.reshape(1, 128)
    message = pack(grad, gate_probs.T, routing.T, old, new, shared_hidden, shared_weight)
    message = exchange(message, "expert")
    terms = hidden_terms(message, old_weights.swapaxes(1, 2), grad)
    terms = partial_sum(exchange(terms, ("z_lo", "x_hi")))
    weight_grad, shared_weight_grad = weight_terms(message, saved_hidden)
    pieces, shared_hidden_grad = spread(exchange(terms, "z_hi"))
    pieces = permute(exchange(pieces, "expert"), old, new)
    hidden_grad = gather(exchange(pieces, "expert"))
    return (
        weight_grad.swapaxes(1, 2),
        hidden_grad.swapaxes(0, 1),
        shared_hidden_grad.T,
        shared_weight_grad,
    )


def solution(mesh):
    dp = ("z_hi", "z_lo", "x_hi")
    finer = Mesh(mesh.devices.reshape(8, 2, 2, mesh.shape["expert"]), (*dp, "expert"))
    return jax.shard_map(
        on_device,
        mesh=finer,
        in_specs=(
            P("expert", dp),
            P("expert", None),
            P("expert", None),
            P("expert", None, dp),
            P(),
            P(),
            P("expert", None, None),
            P("expert", None),
            P("expert", dp),
        ),
        out_specs=(P("expert", None, dp), P("expert", dp, None), P("expert", dp), P("expert", dp)),
        check_vma=False,
    )
```

```python
import functools

import jax
import jax.numpy as jnp
from jax import lax
from jax.experimental import pallas as pl
from jax.experimental.pallas import tpu as pltpu
from jax.sharding import Mesh
from jax.sharding import PartitionSpec as P

F32, BF16, I32 = jnp.float32, jnp.bfloat16, jnp.int32
INTERPRET = False

MESSAGE = 120
DP = ("z_hi", "z_lo", "x_hi")
EXPERT = ("x_lo", "y2", "y1", "y0", "core")


def iota(shape, dim):
    return lax.broadcasted_iota(I32, shape, dim)


def dot(a, b, a_dim=1, b_dim=0):
    return lax.dot_general(a, b, (((a_dim,), (b_dim,)), ((), ())), preferred_element_type=F32)


def call(body, out, *args, flops=0, held=()):
    outs = out if isinstance(out, tuple) else (out,)
    moved = sum(x.size * x.dtype.itemsize for x in (*args, *outs))
    in_vmem, anywhere = pl.BlockSpec(memory_space=pltpu.VMEM), pl.BlockSpec()
    args = [
        pltpu.with_memory_space_constraint(x, pltpu.VMEM) if i in held else x
        for i, x in enumerate(args)
    ]
    return pl.pallas_call(
        body,
        out_shape=out,
        in_specs=[in_vmem if i in held else anywhere for i in range(len(args))],
        interpret=INTERPRET,
        cost_estimate=pl.CostEstimate(flops=flops, bytes_accessed=moved, transcendentals=0),
    )(*args)


def tails(grad):
    low = grad[128:192, :]
    none = jnp.zeros((64, 128), BF16)
    return jnp.concatenate([low, none], axis=0), jnp.concatenate([none, low], axis=0)


def pack_body(grad_ref, gate_ref, routing_ref, old_ref, new_ref, weight_ref, out_ref):
    grad = grad_ref[...]
    first, last = tails(grad)
    head = grad[0:128, :]
    wide = (32, 24, 128)
    flat = (768, 128)
    row, lane = iota(wide, 1), iota(wide, 2)
    slot = iota(wide, 0) * 4 + lax.bitwise_and(row, 3)
    pick = jnp.where(lane == slot, 1.0, 0.0).astype(F32).reshape(flat).astype(BF16)
    rank_of_row = lax.shift_right_logical(row, 2).astype(F32).reshape(flat)
    before = jnp.where(iota((128, 128), 0) < iota((128, 128), 1), 1.0, 0.0).astype(BF16)
    routing = routing_ref[...].astype(F32)
    gates = gate_ref[...]

    def rows_for(listing_ref):
        listing = jnp.broadcast_to(listing_ref[...].astype(F32), (128, 128)).astype(BF16)
        expert = dot(pick, listing, 1, 1)
        named = jnp.zeros(flat, F32)
        gate = jnp.zeros(flat, F32)
        for k in range(4):
            match = expert == routing[k : k + 1, :]
            named = jnp.where(match, 1.0, named)
            gate = jnp.where(match, gates[k : k + 1, :], gate)
        rank = dot(named.astype(BF16), before)
        chosen = jnp.logical_and(named > 0.5, rank == rank_of_row)
        select = jnp.where(chosen, 1.0, 0.0).astype(BF16)
        scale = jnp.sum(jnp.where(chosen, gate, 0.0), axis=1, keepdims=True)
        return select, scale

    old_select, old_scale = rows_for(old_ref)
    new_select, new_scale = rows_for(new_ref)
    old_rows = (dot(old_select, head, 1, 1) * old_scale).reshape(wide)
    new_rows = (dot(new_select, head, 1, 1) * new_scale).reshape(wide)
    out_ref[:, 0:48, :] = jnp.concatenate([old_rows, new_rows], axis=1).astype(BF16)
    rest = dot(old_select, first, 1, 1) * old_scale + dot(new_select, last, 1, 1) * new_scale
    out_ref[:, 96:120, :] = rest.reshape(wide).astype(BF16)
    weight = weight_ref[...]
    out_ref[:, 48:80, :] = jnp.broadcast_to(weight[None, :, 0:128], (32, 32, 128))
    both = jnp.concatenate([weight[0:16, 128:192], weight[16:32, 128:192]], axis=1)
    out_ref[:, 80:96, :] = jnp.broadcast_to(both[None], (32, 16, 128))


def position(axis):
    return lax.axis_index(axis)


def shared_body(hidden_ref, grad_ref, keep_ref, send_ref, terms_ref):
    grad = grad_ref[...]
    first, last = tails(grad)
    hidden = hidden_ref[...]
    terms_ref[:, :, 0:32, :] = dot(hidden, grad[0:128, :], 0, 1).reshape(16, 2, 32, 128)
    low = dot(hidden, first, 0, 1).reshape(32, 32, 128)[:, 0:16]
    high = dot(hidden, last, 0, 1).reshape(32, 32, 128)[:, 16:32]
    terms_ref[:, :, 32:48, :] = (low + high).reshape(16, 2, 16, 128)
    mine = position("core")
    keep_ref[...] = terms_ref[:, mine]
    send_ref[...] = terms_ref[:, 1 - mine].astype(BF16)


def halve_body(axis, keep_ref, received_ref, next_ref, send_ref):
    mine = position(axis)
    other = 1 - mine
    next_ref[...] = keep_ref[:, mine] + received_ref[:, mine].astype(F32)
    send_ref[...] = (keep_ref[:, other] + received_ref[:, other].astype(F32)).astype(BF16)


def finish_body(keep_ref, received_ref, out_ref):
    total = keep_ref[0] + received_ref[0].astype(F32)
    out_ref[:, 0:128] = total[0:32].astype(BF16)
    tail = jnp.concatenate([total[32:48, 0:64], pltpu.roll(total[32:48], 64, 1)[:, 0:64]], axis=0)
    out_ref[:, 128:192] = tail.astype(BF16)


def hidden_body(message_ref, old_weights_ref, grad_ref, out_ref, new_ref):
    m = pl.program_id(0)

    def part(start, stop):
        return jnp.stack([message_ref[z * 4 + m, start:stop, :] for z in range(8)])

    grad = grad_ref[...]
    first, last = tails(grad)
    lane = iota((192, 128), 1)
    left = lane < 64
    own = lax.bitwise_and(iota((8, 24, 128), 1), 3).reshape(192, 128)
    wide = (8, 24, 256)
    row = iota(wide, 1) - 20
    where_to = iota(wide, 2) - iota(wide, 0) * 32 - row * 8
    where_to = jnp.where(row >= 0, where_to, -1).reshape(192, 256)
    heads = part(0, 48).astype(F32)
    rest = part(96, 120).astype(F32)
    new_ref[:, 0] = jnp.concatenate([heads[:, 24:48], rest], axis=1).astype(BF16)
    heads = heads[:, 0:24].reshape(192, 128)
    rest = rest.reshape(192, 128)
    heads_turned = pltpu.roll(heads, 64, 1)
    rest_turned = pltpu.roll(rest, 64, 1)
    blocks = []
    for e in (0, 2):
        blocks.append(jnp.where(own == e, heads, 0.0))
        blocks.append(
            jnp.where(
                left, jnp.where(own == e, rest, 0.0), jnp.where(own == e + 1, heads_turned, 0.0)
            )
        )
        blocks.append(jnp.where(own == e + 1, jnp.where(left, heads_turned, rest_turned), 0.0))
    rows = jnp.concatenate(blocks, axis=1).astype(BF16)
    total = dot(rows, old_weights_ref[...].reshape(768, 1024))
    units = dot(part(48, 80).reshape(256, 128), grad[0:128, :]).reshape(8, 32, 128)
    pairs = part(80, 96).reshape(128, 128)
    low, high = dot(pairs, first).reshape(8, 16, 128), dot(pairs, last).reshape(8, 16, 128)
    units = units + jnp.concatenate([low, high], axis=1)
    shared = units.reshape(256, 128).astype(BF16)
    placed = [dot(jnp.where(where_to == j, 1.0, 0.0).astype(BF16), shared) for j in range(8)]
    total = total + jnp.concatenate(placed, axis=1)
    out_ref[0] = total.reshape(8, 24, 1024).astype(BF16)


def weight_body(rows_ref, saved_ref, out_ref):
    rows = rows_ref[...].astype(F32)
    heads = rows[:, 0:24].reshape(768, 128)
    rest = rows[:, 24:48].reshape(768, 128)
    rows = jnp.concatenate([heads, rest], axis=1).astype(BF16)
    line, place = iota((160, 768), 0), iota((160, 768), 1)
    group = lax.shift_right_logical(line * 205, 10)
    start = (line + group) * 4

    def step(e, carry):
        match = jnp.where(place == start + e, 1.0, 0.0).astype(BF16)
        own = dot(match, rows).astype(BF16)
        product = dot(own, saved_ref[e], 0, 0).astype(BF16)
        out_ref[e, 0:128, :] = product[0:128]
        out_ref[e, 128:192, :] = product[192:256]
        return carry

    lax.fori_loop(0, 4, step, 0)


def spread_body(in_ref, out_ref, shared_ref):
    total = jnp.sum(in_ref[...].astype(F32), axis=0)
    for c in range(5):
        for h in range(4):
            piece = total[c * 4 : c * 4 + 4]
            at = h * 256
            both = jnp.concatenate([piece[:, at : at + 128], piece[:, at + 128 : at + 256]], axis=0)
            out_ref[c * 4 + h] = both.astype(BF16)
    out_ref[20:32] = jnp.zeros((12, 8, 128), BF16)
    units = [
        total[20 + r : 21 + r, j * 128 : (j + 1) * 128] for r in range(4) for j in range(8)
    ]
    shared_ref[...] = jnp.concatenate(units, axis=0).astype(BF16)


def match_body(old_ref, new_ref, out_ref):
    line, lane = iota((256, 128), 0), iota((256, 128), 1)
    slot = lax.shift_right_logical(line, 3) * 4 + lax.bitwise_and(line, 3)
    pick = jnp.where(lane == slot, 1.0, 0.0)
    wide = jnp.broadcast_to(new_ref[...].astype(F32), (256, 128)).astype(BF16)
    to = dot(pick.astype(BF16), wide, 1, 1)
    mine = jnp.broadcast_to(old_ref[...].astype(F32), (256, 128)).astype(BF16)
    source = dot(mine, pick.astype(BF16), 1, 1)
    side = lax.bitwise_and(iota((256, 256), 0), 4) == lax.bitwise_and(iota((256, 256), 1), 4)
    out_ref[...] = jnp.where(jnp.logical_and(to == source, side), 1.0, 0.0).astype(BF16)


def permute_body(in_ref, match_ref, out_ref):
    moved = dot(match_ref[...], in_ref[...].reshape(256, 128))
    out_ref[...] = moved.reshape(32, 8, 128).astype(BF16)


def shaped(dtype, *shape):
    return jax.ShapeDtypeStruct(shape, dtype)


def pack(grad, gates, routing, old, new, weight):
    out = shaped(BF16, 32, MESSAGE, 128)
    return call(pack_body, out, grad, gates, routing, old, new, weight, flops=10**9)


def hidden_terms(message, weights, grad):
    out = (shaped(BF16, 4, 8, 24, 1024), shaped(BF16, 8, 4, 48, 128))
    moved = sum(x.size * 2 for x in (message, weights, grad, *out))
    return pl.pallas_call(
        hidden_body,
        grid=(4,),
        in_specs=[pl.BlockSpec(memory_space=pltpu.VMEM)] * 3,
        out_specs=(
            pl.BlockSpec((1, 8, 24, 1024), lambda m: (m, 0, 0, 0)),
            pl.BlockSpec((8, 1, 48, 128), lambda m: (0, m, 0, 0)),
        ),
        out_shape=out,
        interpret=INTERPRET,
        compiler_params=pltpu.CompilerParams(vmem_limit_bytes=40 << 20),
        cost_estimate=pl.CostEstimate(flops=2 * 10**9, bytes_accessed=moved, transcendentals=0),
    )(*(pltpu.with_memory_space_constraint(x, pltpu.VMEM) for x in (message, weights, grad)))


def weight_terms(rows, saved):
    out = shaped(BF16, 4, 192, 1024)
    return call(weight_body, out, rows.reshape(32, 48, 128), saved, flops=10**9)


def partial_sum(received):
    return jnp.sum(received.astype(F32), axis=0).astype(BF16)


def spread(received):
    return call(spread_body, (shaped(BF16, 32, 8, 128), shaped(BF16, 32, 128)), received, held=(0,))


def permute(received, match):
    return call(permute_body, shaped(BF16, 32, 8, 128), received, match, held=(0,))


def gather(received):
    pieces = received[0:20].reshape(5, 4, 2, 4, 128)
    return jnp.transpose(pieces, (0, 3, 1, 2, 4)).reshape(5, 4, 1024)


def exchange(array, axes):
    return lax.all_to_all(array, axes, 0, 0, tiled=True)


def swap(array, axis):
    return lax.ppermute(array, axis, [(0, 1), (1, 0)])


def shared_terms(hidden, grad):
    out = (shaped(F32, 16, 48, 128), shaped(BF16, 16, 48, 128))
    return pl.pallas_call(
        shared_body,
        out_shape=out,
        scratch_shapes=[pltpu.VMEM((16, 2, 48, 128), F32)],
        interpret=INTERPRET,
        cost_estimate=pl.CostEstimate(flops=10**8, bytes_accessed=1 << 20, transcendentals=0),
    )(hidden, grad)


def halve(axis, above, below, keep, received):
    whole = (above, 2, below * 48, 128)
    half = (above, below * 48, 128)
    return call(
        functools.partial(halve_body, axis),
        (shaped(F32, *half), shaped(BF16, *half)),
        keep.reshape(whole),
        received.reshape(whole),
        held=(1,),
    )


def shared_weight_sum(hidden, grad):
    keep, send = shared_terms(hidden, grad)
    last = "core"
    for axis, above, below in (("x_lo", 1, 8), ("y0", 4, 1), ("y1", 2, 1), ("y2", 1, 1)):
        send = swap(send, last)
        keep, send = halve(axis, above, below, keep, send)
        last = axis
    send = swap(send, last)
    return call(finish_body, shaped(BF16, 32, 192), keep, send, held=(1,))


def on_device(
    grad_output,
    gate_probs,
    routing,
    old_weights,
    old_slot_expert,
    new_slot_expert,
    saved_hidden,
    shared_hidden,
    shared_weight,
):
    grad = grad_output.T
    old, new = old_slot_expert.reshape(1, 128), new_slot_expert.reshape(1, 128)
    message = pack(grad, gate_probs.T, routing.T, old, new, shared_weight)
    message = exchange(message, EXPERT)
    shared_weight_grad = shared_weight_sum(shared_hidden, grad)
    match = call(match_body, shaped(BF16, 256, 256), old, new, flops=10**7)
    terms, new_rows = hidden_terms(message, old_weights.swapaxes(1, 2), grad)
    terms = exchange(terms, ("z_lo", "x_hi"))
    terms = partial_sum(terms)
    terms = exchange(terms, "z_hi")
    pieces, shared_hidden_grad = spread(terms)
    pieces = exchange(pieces, EXPERT)
    pieces = permute(pieces, match)
    weight_grad = weight_terms(new_rows, saved_hidden)
    pieces = exchange(pieces, EXPERT)
    hidden_grad = gather(pieces)
    return (
        weight_grad.swapaxes(1, 2),
        hidden_grad.swapaxes(0, 1),
        shared_hidden_grad.T,
        shared_weight_grad,
    )


def solution(mesh):
    finer = Mesh(mesh.devices.reshape(8, *(2,) * 7), (*DP, *EXPERT))
    return jax.shard_map(
        on_device,
        mesh=finer,
        in_specs=(
            P(EXPERT, DP),
            P(EXPERT, None),
            P(EXPERT, None),
            P(EXPERT, None, DP),
            P(),
            P(),
            P(EXPERT, None, None),
            P(EXPERT, None),
            P(EXPERT, DP),
        ),
        out_specs=(P(EXPERT, None, DP), P(EXPERT, DP, None), P(EXPERT, DP), P(EXPERT, DP)),
        check_vma=False,
    )
```

```python
import functools

import jax
import jax.numpy as jnp
from jax import lax
from jax.experimental import pallas as pl
from jax.experimental.pallas import tpu as pltpu
from jax.sharding import Mesh
from jax.sharding import PartitionSpec as P

F32, BF16, I32 = jnp.float32, jnp.bfloat16, jnp.int32
INTERPRET = False

MESSAGE = 88
SECOND = 48
DP = ("z_hi", "z_lo", "x_hi")
EXPERT = ("x_lo", "y2", "y1", "y0", "core")


def iota(shape, dim):
    return lax.broadcasted_iota(I32, shape, dim)


def dot(a, b, a_dim=1, b_dim=0):
    return lax.dot_general(a, b, (((a_dim,), (b_dim,)), ((), ())), preferred_element_type=F32)


def call(body, out, *args, flops=0, held=()):
    outs = out if isinstance(out, tuple) else (out,)
    moved = sum(x.size * x.dtype.itemsize for x in (*args, *outs))
    in_vmem, anywhere = pl.BlockSpec(memory_space=pltpu.VMEM), pl.BlockSpec()
    args = [
        pltpu.with_memory_space_constraint(x, pltpu.VMEM) if i in held else x
        for i, x in enumerate(args)
    ]
    return pl.pallas_call(
        body,
        out_shape=out,
        in_specs=[in_vmem if i in held else anywhere for i in range(len(args))],
        interpret=INTERPRET,
        cost_estimate=pl.CostEstimate(flops=flops, bytes_accessed=moved, transcendentals=0),
    )(*args)


def tails(grad):
    low = grad[128:192, :]
    none = jnp.zeros((64, 128), BF16)
    return jnp.concatenate([low, none], axis=0), jnp.concatenate([none, low], axis=0)


def pack_rows(grad_ref, gate_ref, routing_ref, listing_ref):
    grad = grad_ref[...]
    first, last = tails(grad)
    wide = (32, 24, 128)
    flat = (768, 128)
    row, lane = iota(wide, 1), iota(wide, 2)
    slot = iota(wide, 0) * 4 + lax.bitwise_and(row, 3)
    pick = jnp.where(lane == slot, 1.0, 0.0).astype(F32).reshape(flat).astype(BF16)
    rank_of_row = lax.shift_right_logical(row, 2).astype(F32).reshape(flat)
    before = jnp.where(iota((128, 128), 0) < iota((128, 128), 1), 1.0, 0.0).astype(BF16)
    routing = routing_ref[...].astype(F32)
    gates = gate_ref[...]
    listing = jnp.broadcast_to(listing_ref[...].astype(F32), (128, 128)).astype(BF16)
    expert = dot(pick, listing, 1, 1)
    named = jnp.zeros(flat, F32)
    gate = jnp.zeros(flat, F32)
    for k in range(4):
        match = expert == routing[k : k + 1, :]
        named = jnp.where(match, 1.0, named)
        gate = jnp.where(match, gates[k : k + 1, :], gate)
    rank = dot(named.astype(BF16), before)
    chosen = jnp.logical_and(named > 0.5, rank == rank_of_row)
    select = jnp.where(chosen, 1.0, 0.0).astype(BF16)
    scale = jnp.sum(jnp.where(chosen, gate, 0.0), axis=1, keepdims=True)
    heads = (dot(select, grad[0:128, :], 1, 1) * scale).reshape(wide)
    low = (dot(select, first, 1, 1) * scale).reshape(wide)
    high = (dot(select, last, 1, 1) * scale).reshape(wide)
    rest = jnp.concatenate([low[:, 0:8] + high[:, 16:24], low[:, 8:16]], axis=1)
    return heads.astype(BF16), rest.astype(BF16)


def unpack_rest(rest):
    turned = pltpu.roll(rest[:, 0:8].reshape(-1, 128), 64, 1).reshape(-1, 8, 128)
    return jnp.concatenate([rest, turned], axis=1)


def pack_body(grad_ref, gate_ref, routing_ref, old_ref, weight_ref, out_ref):
    heads, rest = pack_rows(grad_ref, gate_ref, routing_ref, old_ref)
    out_ref[:, 0:24, :] = heads
    out_ref[:, 24:40, :] = rest
    weight = weight_ref[...]
    out_ref[:, 40:72, :] = jnp.broadcast_to(weight[None, :, 0:128], (32, 32, 128))
    both = jnp.concatenate([weight[0:16, 128:192], weight[16:32, 128:192]], axis=1)
    out_ref[:, 72:88, :] = jnp.broadcast_to(both[None], (32, 16, 128))


def pack_new_body(grad_ref, gate_ref, routing_ref, new_ref, out_ref):
    heads, rest = pack_rows(grad_ref, gate_ref, routing_ref, new_ref)
    out_ref[:, 0:24, :] = heads
    out_ref[:, 24:40, :] = rest


def position(axis):
    return lax.axis_index(axis)


def shared_body(hidden_ref, grad_ref, keep_ref, send_ref, terms_ref):
    grad = grad_ref[...]
    first, last = tails(grad)
    hidden = hidden_ref[...]
    terms_ref[:, :, 0:32, :] = dot(hidden, grad[0:128, :], 0, 1).reshape(16, 2, 32, 128)
    low = dot(hidden, first, 0, 1).reshape(32, 32, 128)[:, 0:16]
    high = dot(hidden, last, 0, 1).reshape(32, 32, 128)[:, 16:32]
    terms_ref[:, :, 32:48, :] = (low + high).reshape(16, 2, 16, 128)
    mine = position("core")
    keep_ref[...] = terms_ref[:, mine]
    send_ref[...] = terms_ref[:, 1 - mine].astype(BF16)


def halve_body(axis, keep_ref, received_ref, next_ref, send_ref):
    mine = position(axis)
    other = 1 - mine
    next_ref[...] = keep_ref[:, mine] + received_ref[:, mine].astype(F32)
    send_ref[...] = (keep_ref[:, other] + received_ref[:, other].astype(F32)).astype(BF16)


def finish_body(keep_ref, received_ref, out_ref):
    total = keep_ref[0] + received_ref[0].astype(F32)
    out_ref[:, 0:128] = total[0:32].astype(BF16)
    tail = jnp.concatenate([total[32:48, 0:64], pltpu.roll(total[32:48], 64, 1)[:, 0:64]], axis=0)
    out_ref[:, 128:192] = tail.astype(BF16)


def hidden_body(message_ref, old_weights_ref, grad_ref, out_ref):
    m = pl.program_id(0)

    def part(start, stop):
        return jnp.stack([message_ref[z * 4 + m, start:stop, :] for z in range(8)])

    grad = grad_ref[...]
    first, last = tails(grad)
    lane = iota((192, 128), 1)
    left = lane < 64
    own = lax.bitwise_and(iota((8, 24, 128), 1), 3).reshape(192, 128)
    wide = (8, 24, 256)
    row = iota(wide, 1) - 20
    where_to = iota(wide, 2) - iota(wide, 0) * 32 - row * 8
    where_to = jnp.where(row >= 0, where_to, -1).reshape(192, 256)
    heads = part(0, 24).astype(F32).reshape(192, 128)
    rest = unpack_rest(part(24, 40).astype(F32)).reshape(192, 128)
    heads_turned = pltpu.roll(heads, 64, 1)
    rest_turned = pltpu.roll(rest, 64, 1)
    blocks = []
    for e in (0, 2):
        blocks.append(jnp.where(own == e, heads, 0.0))
        blocks.append(
            jnp.where(
                left, jnp.where(own == e, rest, 0.0), jnp.where(own == e + 1, heads_turned, 0.0)
            )
        )
        blocks.append(jnp.where(own == e + 1, jnp.where(left, heads_turned, rest_turned), 0.0))
    rows = jnp.concatenate(blocks, axis=1).astype(BF16)
    total = dot(rows, old_weights_ref[...].reshape(768, 1024))
    units = dot(part(40, 72).reshape(256, 128), grad[0:128, :]).reshape(8, 32, 128)
    pairs = part(72, 88).reshape(128, 128)
    low, high = dot(pairs, first).reshape(8, 16, 128), dot(pairs, last).reshape(8, 16, 128)
    units = units + jnp.concatenate([low, high], axis=1)
    shared = units.reshape(256, 128).astype(BF16)
    placed = [dot(jnp.where(where_to == j, 1.0, 0.0).astype(BF16), shared) for j in range(8)]
    total = total + jnp.concatenate(placed, axis=1)
    out_ref[0] = total.reshape(8, 24, 1024).astype(BF16)


def weight_body(rows_ref, saved_ref, out_ref):
    rows = rows_ref[:, 8:48, :].astype(F32)
    heads = rows[:, 0:24].reshape(768, 128)
    rest = unpack_rest(rows[:, 24:40]).reshape(768, 128)
    rows = jnp.concatenate([heads, rest], axis=1).astype(BF16)
    line, place = iota((160, 768), 0), iota((160, 768), 1)
    group = lax.shift_right_logical(line * 205, 10)
    start = (line + group) * 4

    def step(e, carry):
        match = jnp.where(place == start + e, 1.0, 0.0).astype(BF16)
        own = dot(match, rows).astype(BF16)
        product = dot(own, saved_ref[e], 0, 0).astype(BF16)
        out_ref[e] = product[0:192]
        return carry

    lax.fori_loop(0, 4, step, 0)


def spread_body(in_ref, rows_ref, out_ref, shared_ref):
    out_ref[:, 8:48, :] = rows_ref[...]
    total = jnp.sum(in_ref[...].astype(F32), axis=0)
    for c in range(5):
        for h in range(4):
            piece = total[c * 4 : c * 4 + 4]
            at = h * 256
            both = jnp.concatenate([piece[:, at : at + 128], piece[:, at + 128 : at + 256]], axis=0)
            out_ref[c * 4 + h, 0:8, :] = both.astype(BF16)
    out_ref[20:32, 0:8, :] = jnp.zeros((12, 8, 128), BF16)
    units = [
        total[20 + r : 21 + r, j * 128 : (j + 1) * 128] for r in range(4) for j in range(8)
    ]
    shared_ref[...] = jnp.concatenate(units, axis=0).astype(BF16)


def match_body(old_ref, new_ref, out_ref):
    line, lane = iota((256, 128), 0), iota((256, 128), 1)
    slot = lax.shift_right_logical(line, 3) * 4 + lax.bitwise_and(line, 3)
    pick = jnp.where(lane == slot, 1.0, 0.0)
    wide = jnp.broadcast_to(new_ref[...].astype(F32), (256, 128)).astype(BF16)
    to = dot(pick.astype(BF16), wide, 1, 1)
    mine = jnp.broadcast_to(old_ref[...].astype(F32), (256, 128)).astype(BF16)
    source = dot(mine, pick.astype(BF16), 1, 1)
    side = lax.bitwise_and(iota((256, 256), 0), 4) == lax.bitwise_and(iota((256, 256), 1), 4)
    out_ref[...] = jnp.where(jnp.logical_and(to == source, side), 1.0, 0.0).astype(BF16)


def permute_body(in_ref, match_ref, out_ref):
    moved = dot(match_ref[...], in_ref[:, 0:8, :].reshape(256, 128))
    out_ref[...] = moved.reshape(32, 8, 128).astype(BF16)


def shaped(dtype, *shape):
    return jax.ShapeDtypeStruct(shape, dtype)


def pack(grad, gates, routing, old, weight):
    out = shaped(BF16, 32, MESSAGE, 128)
    return call(pack_body, out, grad, gates, routing, old, weight, flops=10**9)


def pack_new(grad, gates, routing, new):
    out = shaped(BF16, 32, SECOND - 8, 128)
    return call(pack_new_body, out, grad, gates, routing, new, flops=10**9)


def hidden_terms(message, weights, grad):
    out = shaped(BF16, 4, 8, 24, 1024)
    moved = sum(x.size * 2 for x in (message, weights, grad, out))
    return pl.pallas_call(
        hidden_body,
        grid=(4,),
        in_specs=[pl.BlockSpec(memory_space=pltpu.VMEM)] * 3,
        out_specs=pl.BlockSpec((1, 8, 24, 1024), lambda m: (m, 0, 0, 0)),
        out_shape=out,
        interpret=INTERPRET,
        compiler_params=pltpu.CompilerParams(vmem_limit_bytes=40 << 20),
        cost_estimate=pl.CostEstimate(flops=2 * 10**9, bytes_accessed=moved, transcendentals=0),
    )(*(pltpu.with_memory_space_constraint(x, pltpu.VMEM) for x in (message, weights, grad)))


def weight_terms(rows, saved):
    out = shaped(BF16, 4, 192, 1024)
    return call(weight_body, out, rows, saved, flops=10**9, held=(0,))


def partial_sum(received):
    return jnp.sum(received.astype(F32), axis=0).astype(BF16)


def spread(received, rows):
    out = (shaped(BF16, 32, SECOND, 128), shaped(BF16, 32, 128))
    return call(spread_body, out, received, rows, held=(0, 1))


def permute(received, match):
    return call(permute_body, shaped(BF16, 32, 8, 128), received, match, held=(0,))


def gather(received):
    pieces = received[0:20].reshape(5, 4, 2, 4, 128)
    return jnp.transpose(pieces, (0, 3, 1, 2, 4)).reshape(5, 4, 1024)


def exchange(array, axes):
    return lax.all_to_all(array, axes, 0, 0, tiled=True)


def swap(array, axis):
    return lax.ppermute(array, axis, [(0, 1), (1, 0)])


def shared_terms(hidden, grad):
    out = (shaped(F32, 16, 48, 128), shaped(BF16, 16, 48, 128))
    return pl.pallas_call(
        shared_body,
        out_shape=out,
        scratch_shapes=[pltpu.VMEM((16, 2, 48, 128), F32)],
        interpret=INTERPRET,
        cost_estimate=pl.CostEstimate(flops=10**8, bytes_accessed=1 << 20, transcendentals=0),
    )(hidden, grad)


def halve(axis, above, below, keep, received):
    whole = (above, 2, below * 48, 128)
    half = (above, below * 48, 128)
    return call(
        functools.partial(halve_body, axis),
        (shaped(F32, *half), shaped(BF16, *half)),
        keep.reshape(whole),
        received.reshape(whole),
        held=(1,),
    )


def shared_weight_sum(hidden, grad):
    keep, send = shared_terms(hidden, grad)
    last = "core"
    for axis, above, below in (("x_lo", 1, 8), ("y0", 4, 1), ("y1", 2, 1), ("y2", 1, 1)):
        send = swap(send, last)
        keep, send = halve(axis, above, below, keep, send)
        last = axis
    send = swap(send, last)
    return call(finish_body, shaped(BF16, 32, 192), keep, send, held=(1,))


def on_device(
    grad_output,
    gate_probs,
    routing,
    old_weights,
    old_slot_expert,
    new_slot_expert,
    saved_hidden,
    shared_hidden,
    shared_weight,
):
    grad = grad_output.T
    old, new = old_slot_expert.reshape(1, 128), new_slot_expert.reshape(1, 128)
    message = pack(grad, gate_probs.T, routing.T, old, shared_weight)
    message = exchange(message, EXPERT)
    new_rows = pack_new(grad, gate_probs.T, routing.T, new)
    shared_weight_grad = shared_weight_sum(shared_hidden, grad)
    match = call(match_body, shaped(BF16, 256, 256), old, new, flops=10**7)
    terms = hidden_terms(message, old_weights.swapaxes(1, 2), grad)
    terms = exchange(terms, ("z_lo", "x_hi"))
    terms = partial_sum(terms)
    terms = exchange(terms, "z_hi")
    second, shared_hidden_grad = spread(terms, new_rows)
    second = exchange(second, EXPERT)
    pieces = permute(second, match)
    weight_grad = weight_terms(second, saved_hidden)
    pieces = exchange(pieces, EXPERT)
    hidden_grad = gather(pieces)
    return (
        weight_grad.swapaxes(1, 2),
        hidden_grad.swapaxes(0, 1),
        shared_hidden_grad.T,
        shared_weight_grad,
    )


def solution(mesh):
    finer = Mesh(mesh.devices.reshape(8, *(2,) * 7), (*DP, *EXPERT))
    return jax.shard_map(
        on_device,
        mesh=finer,
        in_specs=(
            P(EXPERT, DP),
            P(EXPERT, None),
            P(EXPERT, None),
            P(EXPERT, None, DP),
            P(),
            P(),
            P(EXPERT, None, None),
            P(EXPERT, None),
            P(EXPERT, DP),
        ),
        out_specs=(P(EXPERT, None, DP), P(EXPERT, DP, None), P(EXPERT, DP), P(EXPERT, DP)),
        check_vma=False,
    )
```

```python
import functools

import jax
import jax.numpy as jnp
from jax import lax
from jax.experimental import pallas as pl
from jax.experimental.pallas import tpu as pltpu
from jax.sharding import Mesh
from jax.sharding import PartitionSpec as P

F32, BF16, I32 = jnp.float32, jnp.bfloat16, jnp.int32
INTERPRET = False

MESSAGE = 80
SECOND = 48
DP = ("z_hi", "z_lo", "x_hi")
EXPERT = ("x_lo", "y2", "y1", "y0", "core")


def iota(shape, dim):
    return lax.broadcasted_iota(I32, shape, dim)


def dot(a, b, a_dim=1, b_dim=0):
    return lax.dot_general(a, b, (((a_dim,), (b_dim,)), ((), ())), preferred_element_type=F32)


def call(body, out, *args, flops=0, held=()):
    outs = out if isinstance(out, tuple) else (out,)
    moved = sum(x.size * x.dtype.itemsize for x in (*args, *outs))
    in_vmem, anywhere = pl.BlockSpec(memory_space=pltpu.VMEM), pl.BlockSpec()
    args = [
        pltpu.with_memory_space_constraint(x, pltpu.VMEM) if i in held else x
        for i, x in enumerate(args)
    ]
    return pl.pallas_call(
        body,
        out_shape=out,
        in_specs=[in_vmem if i in held else anywhere for i in range(len(args))],
        interpret=INTERPRET,
        cost_estimate=pl.CostEstimate(flops=flops, bytes_accessed=moved, transcendentals=0),
    )(*args)


def tails(grad):
    low = grad[128:192, :]
    none = jnp.zeros((64, 128), BF16)
    return jnp.concatenate([low, none], axis=0), jnp.concatenate([none, low], axis=0)


def pack_rows(grad_ref, gate_ref, routing_ref, listing_ref, ends=None):
    grad = grad_ref[...]
    first, last = tails(grad)
    wide = (32, 24, 128)
    flat = (768, 128)
    row, lane = iota(wide, 1), iota(wide, 2)
    slot = iota(wide, 0) * 4 + lax.bitwise_and(row, 3)
    pick = jnp.where(lane == slot, 1.0, 0.0).astype(F32).reshape(flat).astype(BF16)
    rank_of_row = lax.shift_right_logical(row, 2).astype(F32).reshape(flat)
    before = jnp.where(iota((128, 128), 0) < iota((128, 128), 1), 1.0, 0.0).astype(BF16)
    routing = routing_ref[...].astype(F32)
    gates = gate_ref[...]
    listing = jnp.broadcast_to(listing_ref[...].astype(F32), (128, 128)).astype(BF16)
    expert = dot(pick, listing, 1, 1)
    named = jnp.zeros(flat, F32)
    gate = jnp.zeros(flat, F32)
    for k in range(4):
        match = expert == routing[k : k + 1, :]
        named = jnp.where(match, 1.0, named)
        gate = jnp.where(match, gates[k : k + 1, :], gate)
    rank = dot(named.astype(BF16), before)
    chosen = jnp.logical_and(named > 0.5, rank == rank_of_row)
    select = jnp.where(chosen, 1.0, 0.0).astype(BF16)
    scale = jnp.sum(jnp.where(chosen, gate, 0.0), axis=1, keepdims=True)
    heads = (dot(select, grad[0:128, :], 1, 1) * scale).reshape(wide)
    low = (dot(select, first, 1, 1) * scale).reshape(wide)
    high = (dot(select, last, 1, 1) * scale).reshape(wide)
    upper = low[:, 8:16]
    if ends is not None:
        swapped = jnp.concatenate([ends[4:8], ends[0:4]], axis=1)
        extra = jnp.concatenate([jnp.zeros((4, 128), F32), swapped], axis=0)
        heads = jnp.concatenate([heads[:, 0:16], heads[:, 16:24] + extra[None]], axis=1)
        extra = jnp.concatenate([jnp.zeros((8, 64), F32), ends[8:16]], axis=1)
        upper = upper + extra[None]
    rest = jnp.concatenate([low[:, 0:8] + high[:, 16:24], upper], axis=1)
    return heads.astype(BF16), rest.astype(BF16)


def unpack_rest(rest):
    turned = pltpu.roll(rest[:, 0:8].reshape(-1, 128), 64, 1).reshape(-1, 8, 128)
    return jnp.concatenate([rest, turned], axis=1)


def pack_body(grad_ref, gate_ref, routing_ref, old_ref, weight_ref, out_ref):
    weight = weight_ref[...]
    ends = weight[:, 128:192].astype(F32)
    heads, rest = pack_rows(grad_ref, gate_ref, routing_ref, old_ref, ends)
    out_ref[:, 0:24, :] = heads
    out_ref[:, 24:40, :] = rest
    out_ref[:, 40:72, :] = jnp.broadcast_to(weight[None, :, 0:128], (32, 32, 128))
    both = jnp.concatenate([ends[16:24], ends[24:32]], axis=1).astype(BF16)
    out_ref[:, 72:80, :] = jnp.broadcast_to(both[None], (32, 8, 128))


def pack_new_body(grad_ref, gate_ref, routing_ref, new_ref, out_ref):
    heads, rest = pack_rows(grad_ref, gate_ref, routing_ref, new_ref)
    out_ref[:, 0:24, :] = heads
    out_ref[:, 24:40, :] = rest


def position(axis):
    return lax.axis_index(axis)


def shared_body(hidden_ref, grad_ref, keep_ref, send_ref, terms_ref):
    grad = grad_ref[...]
    first, last = tails(grad)
    hidden = hidden_ref[...]
    terms_ref[:, :, 0:32, :] = dot(hidden, grad[0:128, :], 0, 1).reshape(16, 2, 32, 128)
    low = dot(hidden, first, 0, 1).reshape(32, 32, 128)[:, 0:16]
    high = dot(hidden, last, 0, 1).reshape(32, 32, 128)[:, 16:32]
    terms_ref[:, :, 32:48, :] = (low + high).reshape(16, 2, 16, 128)
    mine = position("core")
    keep_ref[...] = terms_ref[:, mine]
    send_ref[...] = terms_ref[:, 1 - mine].astype(BF16)


def halve_body(axis, keep_ref, received_ref, next_ref, send_ref):
    mine = position(axis)
    other = 1 - mine
    next_ref[...] = keep_ref[:, mine] + received_ref[:, mine].astype(F32)
    send_ref[...] = (keep_ref[:, other] + received_ref[:, other].astype(F32)).astype(BF16)


def finish_body(keep_ref, received_ref, out_ref):
    total = keep_ref[0] + received_ref[0].astype(F32)
    out_ref[:, 0:128] = total[0:32].astype(BF16)
    tail = jnp.concatenate([total[32:48, 0:64], pltpu.roll(total[32:48], 64, 1)[:, 0:64]], axis=0)
    out_ref[:, 128:192] = tail.astype(BF16)


def hidden_body(message_ref, old_weights_ref, grad_ref, out_ref):
    m = pl.program_id(0)

    def part(start, stop):
        return jnp.stack([message_ref[z * 4 + m, start:stop, :] for z in range(8)])

    grad = grad_ref[...]
    first, last = tails(grad)
    lane = iota((192, 128), 1)
    left = lane < 64
    own = iota((8, 24, 128), 1)
    own = jnp.where(own < 20, lax.bitwise_and(own, 3), 4).reshape(192, 128)
    wide = (8, 24, 256)
    row = iota(wide, 1) - 20
    where_to = iota(wide, 2) - iota(wide, 0) * 32 - row * 8
    where_to = jnp.where(row >= 0, where_to, -1).reshape(192, 256)
    heads = part(0, 24).astype(F32)
    rest = part(24, 40).astype(F32)
    ends = jnp.concatenate([heads[:, 16:24], rest[:, 8:16], part(72, 80).astype(F32)], axis=1)
    heads = heads.reshape(192, 128)
    rest = unpack_rest(rest).reshape(192, 128)
    heads_turned = pltpu.roll(heads, 64, 1)
    rest_turned = pltpu.roll(rest, 64, 1)
    blocks = []
    for e in (0, 2):
        blocks.append(jnp.where(own == e, heads, 0.0))
        blocks.append(
            jnp.where(
                left, jnp.where(own == e, rest, 0.0), jnp.where(own == e + 1, heads_turned, 0.0)
            )
        )
        blocks.append(jnp.where(own == e + 1, jnp.where(left, heads_turned, rest_turned), 0.0))
    rows = jnp.concatenate(blocks, axis=1).astype(BF16)
    total = dot(rows, old_weights_ref[...].reshape(768, 1024))
    units = dot(part(40, 72).reshape(256, 128), grad[0:128, :]).reshape(8, 32, 128)
    ends = ends.reshape(192, 128).astype(BF16)
    low, high = dot(ends, first).reshape(8, 24, 128), dot(ends, last).reshape(8, 24, 128)
    ends = [high[:, 4:8], low[:, 4:8], high[:, 8:16], low[:, 16:24], high[:, 16:24]]
    units = units + jnp.concatenate(ends, axis=1)
    shared = units.reshape(256, 128).astype(BF16)
    placed = [dot(jnp.where(where_to == j, 1.0, 0.0).astype(BF16), shared) for j in range(8)]
    total = total + jnp.concatenate(placed, axis=1)
    out_ref[0] = total.reshape(8, 24, 1024).astype(BF16)


def weight_body(rows_ref, saved_ref, out_ref):
    rows = rows_ref[:, 8:48, :].astype(F32)
    heads = rows[:, 0:24].reshape(768, 128)
    rest = unpack_rest(rows[:, 24:40]).reshape(768, 128)
    rows = jnp.concatenate([heads, rest], axis=1).astype(BF16)
    line, place = iota((160, 768), 0), iota((160, 768), 1)
    group = lax.shift_right_logical(line * 205, 10)
    start = (line + group) * 4

    def step(e, carry):
        match = jnp.where(place == start + e, 1.0, 0.0).astype(BF16)
        own = dot(match, rows).astype(BF16)
        product = dot(own, saved_ref[e], 0, 0).astype(BF16)
        out_ref[e] = product[0:192]
        return carry

    lax.fori_loop(0, 4, step, 0)


def spread_body(in_ref, rows_ref, out_ref, shared_ref):
    out_ref[:, 8:48, :] = rows_ref[...]
    total = jnp.sum(in_ref[...].astype(F32), axis=0)
    for c in range(5):
        for h in range(4):
            piece = total[c * 4 : c * 4 + 4]
            at = h * 256
            both = jnp.concatenate([piece[:, at : at + 128], piece[:, at + 128 : at + 256]], axis=0)
            out_ref[c * 4 + h, 0:8, :] = both.astype(BF16)
    out_ref[20:32, 0:8, :] = jnp.zeros((12, 8, 128), BF16)
    units = [
        total[20 + r : 21 + r, j * 128 : (j + 1) * 128] for r in range(4) for j in range(8)
    ]
    shared_ref[...] = jnp.concatenate(units, axis=0).astype(BF16)


def match_body(old_ref, new_ref, out_ref):
    line, lane = iota((256, 128), 0), iota((256, 128), 1)
    slot = lax.shift_right_logical(line, 3) * 4 + lax.bitwise_and(line, 3)
    pick = jnp.where(lane == slot, 1.0, 0.0)
    wide = jnp.broadcast_to(new_ref[...].astype(F32), (256, 128)).astype(BF16)
    to = dot(pick.astype(BF16), wide, 1, 1)
    mine = jnp.broadcast_to(old_ref[...].astype(F32), (256, 128)).astype(BF16)
    source = dot(mine, pick.astype(BF16), 1, 1)
    side = lax.bitwise_and(iota((256, 256), 0), 4) == lax.bitwise_and(iota((256, 256), 1), 4)
    out_ref[...] = jnp.where(jnp.logical_and(to == source, side), 1.0, 0.0).astype(BF16)


def permute_body(in_ref, match_ref, out_ref):
    moved = dot(match_ref[...], in_ref[:, 0:8, :].reshape(256, 128))
    out_ref[...] = moved.reshape(32, 8, 128).astype(BF16)


def shaped(dtype, *shape):
    return jax.ShapeDtypeStruct(shape, dtype)


def pack(grad, gates, routing, old, weight):
    out = shaped(BF16, 32, MESSAGE, 128)
    return call(pack_body, out, grad, gates, routing, old, weight, flops=10**9)


def pack_new(grad, gates, routing, new):
    out = shaped(BF16, 32, SECOND - 8, 128)
    return call(pack_new_body, out, grad, gates, routing, new, flops=10**9)


def hidden_terms(message, weights, grad):
    out = shaped(BF16, 4, 8, 24, 1024)
    moved = sum(x.size * 2 for x in (message, weights, grad, out))
    return pl.pallas_call(
        hidden_body,
        grid=(4,),
        in_specs=[pl.BlockSpec(memory_space=pltpu.VMEM)] * 3,
        out_specs=pl.BlockSpec((1, 8, 24, 1024), lambda m: (m, 0, 0, 0)),
        out_shape=out,
        interpret=INTERPRET,
        compiler_params=pltpu.CompilerParams(vmem_limit_bytes=40 << 20),
        cost_estimate=pl.CostEstimate(flops=2 * 10**9, bytes_accessed=moved, transcendentals=0),
    )(*(pltpu.with_memory_space_constraint(x, pltpu.VMEM) for x in (message, weights, grad)))


def weight_terms(rows, saved):
    out = shaped(BF16, 4, 192, 1024)
    return call(weight_body, out, rows, saved, flops=10**9, held=(0,))


def partial_sum(received):
    return jnp.sum(received.astype(F32), axis=0).astype(BF16)


def spread(received, rows):
    out = (shaped(BF16, 32, SECOND, 128), shaped(BF16, 32, 128))
    return call(spread_body, out, received, rows, held=(0, 1))


def permute(received, match):
    return call(permute_body, shaped(BF16, 32, 8, 128), received, match, held=(0, 1))


def gather(received):
    pieces = received[0:20].reshape(5, 4, 2, 4, 128)
    return jnp.transpose(pieces, (0, 3, 1, 2, 4)).reshape(5, 4, 1024)


def exchange(array, axes):
    return lax.all_to_all(array, axes, 0, 0, tiled=True)


def swap(array, axis):
    return lax.ppermute(array, axis, [(0, 1), (1, 0)])


def shared_terms(hidden, grad):
    out = (shaped(F32, 16, 48, 128), shaped(BF16, 16, 48, 128))
    return pl.pallas_call(
        shared_body,
        out_shape=out,
        scratch_shapes=[pltpu.VMEM((16, 2, 48, 128), F32)],
        interpret=INTERPRET,
        cost_estimate=pl.CostEstimate(flops=10**8, bytes_accessed=1 << 20, transcendentals=0),
    )(hidden, grad)


def halve(axis, above, below, keep, received):
    whole = (above, 2, below * 48, 128)
    half = (above, below * 48, 128)
    return call(
        functools.partial(halve_body, axis),
        (shaped(F32, *half), shaped(BF16, *half)),
        keep.reshape(whole),
        received.reshape(whole),
        held=(1,),
    )


def shared_weight_sum(hidden, grad):
    keep, send = shared_terms(hidden, grad)
    last = "core"
    for axis, above, below in (("x_lo", 1, 8), ("y0", 4, 1), ("y1", 2, 1), ("y2", 1, 1)):
        send = swap(send, last)
        keep, send = halve(axis, above, below, keep, send)
        last = axis
    send = swap(send, last)
    return call(finish_body, shaped(BF16, 32, 192), keep, send, held=(1,))


def on_device(
    grad_output,
    gate_probs,
    routing,
    old_weights,
    old_slot_expert,
    new_slot_expert,
    saved_hidden,
    shared_hidden,
    shared_weight,
):
    grad = grad_output.T
    old, new = old_slot_expert.reshape(1, 128), new_slot_expert.reshape(1, 128)
    message = pack(grad, gate_probs.T, routing.T, old, shared_weight)
    message = exchange(message, EXPERT)
    new_rows = pack_new(grad, gate_probs.T, routing.T, new)
    shared_weight_grad = shared_weight_sum(shared_hidden, grad)
    match = call(match_body, shaped(BF16, 256, 256), old, new, flops=10**7)
    terms = hidden_terms(message, old_weights.swapaxes(1, 2), grad)
    terms = exchange(terms, ("z_lo", "x_hi"))
    terms = partial_sum(terms)
    terms = exchange(terms, "z_hi")
    second, shared_hidden_grad = spread(terms, new_rows)
    second = exchange(second, EXPERT)
    pieces = permute(second, match)
    weight_grad = weight_terms(second, saved_hidden)
    pieces = exchange(pieces, EXPERT)
    hidden_grad = gather(pieces)
    return (
        weight_grad.swapaxes(1, 2),
        hidden_grad.swapaxes(0, 1),
        shared_hidden_grad.T,
        shared_weight_grad,
    )


def solution(mesh):
    finer = Mesh(mesh.devices.reshape(8, *(2,) * 7), (*DP, *EXPERT))
    return jax.shard_map(
        on_device,
        mesh=finer,
        in_specs=(
            P(EXPERT, DP),
            P(EXPERT, None),
            P(EXPERT, None),
            P(EXPERT, None, DP),
            P(),
            P(),
            P(EXPERT, None, None),
            P(EXPERT, None),
            P(EXPERT, DP),
        ),
        out_specs=(P(EXPERT, None, DP), P(EXPERT, DP, None), P(EXPERT, DP), P(EXPERT, DP)),
        check_vma=False,
    )
```
